128 devices in a mesh: dp: 8 (over x, core), context: 16 (over z, y).
Axes of the slice: x: 4, y: 4, z: 4, core: 2. Of those that a mesh axis runs over, the one named last changes fastest.
Arguments:
- queries: bfloat16 [8, 5120, 4096], P('dp', 'context'), may hold values from -6 to 6
- keys: bfloat16 [8, 5120, 4096], P('dp', 'context'), may hold values from -6 to 6
- values: bfloat16 [8, 5120, 4096], P('dp', 'context'), may hold values from -6 to 6
- gain: float32 [4096], replicated, may hold values from 0.1 to 1.9
- out_grad: bfloat16 [8, 5120, 4096], P('dp', 'context'), may hold values from -6 to 6
Outputs:
- output: bfloat16 [8, 5120, 4096], P('dp', 'context')
- query_grad: bfloat16 [8, 5120, 4096], P('dp', 'context')
- key_grad: bfloat16 [8, 5120, 4096], P('dp', 'context')
- value_grad: bfloat16 [8, 5120, 4096], P('dp', 'context')
- gain_grad: float32 [4096], replicated
The draws below stay inside these ranges and needn't reach their ends.
All inputs are finite; a program needn't handle non-finite values.
Results may differ from the reference program's by a relative error of at most 0.0064.
Values may be sent and summed in bfloat16 or wider, within the bound.
A program may use at most 192 MiB of HBM per device.

```python
import jax
import jax.numpy as jnp
from jax import lax

HEADS = 32
HD = 128
TOK_DEV = 320
FEAT = 4096
SEQS = 8
LENGTH = 5120
N_CONTEXT = 16


def block_levels(key, extent, shards, smallest, largest):
    factor_of = 1.0
    for axis_at, parts in shards:
        draws = jax.random.uniform(jax.random.fold_in(jax.random.fold_in(key, 6), axis_at), (parts,), jnp.float32, smallest / len(shards), largest / len(shards))
        factor_of = factor_of * jnp.repeat(jnp.exp(draws), extent[axis_at] // parts).reshape((-1,) + (1,) * (len(extent) - 1 - axis_at))
    return factor_of


def gaussian(key, shape, scale, limit, cuts=(), kind=jnp.bfloat16):
    array = scale * jax.random.normal(key, shape, jnp.float32)
    if cuts:
        array = array * block_levels(key, shape, cuts, -0.22, 0.18)
    return jnp.clip(array, -limit, limit).astype(kind)


def setup_inputs(seed: int = 0) -> dict:
    seeds = jax.random.split(jax.random.key(seed), 6)
    return {
        "queries": gaussian(seeds[0], (SEQS, LENGTH, FEAT), 1.0, 6.0, ((0, 8), (1, 16))),
        "keys": gaussian(seeds[1], (SEQS, LENGTH, FEAT), 1.0, 6.0, ((0, 8), (1, 16))),
        "values": gaussian(seeds[2], (SEQS, LENGTH, FEAT), 1.0, 6.0, ((0, 8), (1, 16))),
        "gain": jnp.clip(1.0 + 0.18 * jax.random.normal(seeds[3], (FEAT,), jnp.float32), 0.1, 1.9),
        "out_grad": gaussian(seeds[4], (SEQS, LENGTH, FEAT), 1.0, 6.0, ((0, 8), (1, 16))),
    }


epsilon = 1e-06

def preceding_sum(terms):
    totals = jnp.cumsum(terms, 0)
    return jnp.concatenate([jnp.zeros_like(terms[:1]), totals[:-1]], 0)

def one_sequence(pack, gain):
    query_all, key_all, value_all, grad_all = pack
    shape4 = (N_CONTEXT, TOK_DEV, HEADS, HD)
    local_query_rows = query_all.reshape(shape4).astype(jnp.float32)
    local_key_rows = key_all.reshape(shape4).astype(jnp.float32)
    local_value_rows = value_all.reshape(shape4).astype(jnp.float32)
    causal = lax.broadcasted_iota(jnp.int32, (TOK_DEV, TOK_DEV), 0) >= lax.broadcasted_iota(jnp.int32, (TOK_DEV, TOK_DEV), 1)
    block_state = jnp.einsum('cthk,cthv->chkv', local_key_rows, local_value_rows).astype(jnp.bfloat16)
    prior_state = preceding_sum(block_state.astype(jnp.float32))
    preceding_block = prior_state.astype(jnp.bfloat16).astype(jnp.float32)
    scores = jnp.einsum('cthk,cshk->chts', local_query_rows, local_key_rows)
    attn_weights = jnp.where(causal, scores, 0.0).astype(jnp.bfloat16).astype(jnp.float32)
    mixed_out = jnp.einsum('chts,cshv->cthv', attn_weights, local_value_rows) + jnp.einsum('cthk,chkv->cthv', local_query_rows, preceding_block)
    mixed_out = mixed_out.reshape(N_CONTEXT * TOK_DEV, HEADS * HD)
    inv_rms = lax.rsqrt(lax.optimization_barrier(jnp.mean(mixed_out * mixed_out, -1, keepdims=True)) + epsilon)
    normed = mixed_out * inv_rms
    output = (normed * gain).astype(jnp.bfloat16)
    grad_out = grad_all.astype(jnp.float32)
    gain_part = lax.optimization_barrier(jnp.sum(grad_out * normed, 0))
    scaled = gain * grad_out
    centered_input = lax.optimization_barrier(jnp.mean(scaled * mixed_out, -1, keepdims=True))
    mixed_gradient = (inv_rms * scaled - mixed_out * inv_rms * inv_rms * inv_rms * centered_input).astype(jnp.bfloat16)
    mixed_gradient = mixed_gradient.reshape(shape4).astype(jnp.float32)
    d_weights = jnp.where(causal, jnp.einsum('cthv,cshv->chts', mixed_gradient, local_value_rows), 0.0).astype(jnp.bfloat16).astype(jnp.float32)
    state_grad = jnp.einsum('cthk,cthv->chkv', local_query_rows, mixed_gradient).astype(jnp.bfloat16).astype(jnp.float32)
    later_state = preceding_sum(state_grad[::-1])[::-1]
    following_block = later_state.astype(jnp.bfloat16).astype(jnp.float32)
    query_grad = jnp.einsum('chts,cshk->cthk', d_weights, local_key_rows) + jnp.einsum('cthv,chkv->cthk', mixed_gradient, preceding_block)
    key_grad = jnp.einsum('chts,cthk->cshk', d_weights, local_query_rows) + jnp.einsum('cthv,chkv->cthk', local_value_rows, following_block)
    value_grad = jnp.einsum('chts,cthv->cshv', attn_weights, mixed_gradient) + jnp.einsum('cthk,chkv->cthv', local_key_rows, following_block)
    flat = (N_CONTEXT * TOK_DEV, HEADS * HD)
    return (output, query_grad.reshape(flat).astype(jnp.bfloat16), key_grad.reshape(flat).astype(jnp.bfloat16), value_grad.reshape(flat).astype(jnp.bfloat16), gain_part)

def reference(queries, keys, values, gain, out_grad):
    results = lax.map(lambda pack: one_sequence(pack, gain), (queries, keys, values, out_grad))
    output, query_grad, key_grad, value_grad, gain_parts = results
    return (output, query_grad, key_grad, value_grad, lax.optimization_barrier(jnp.sum(gain_parts, 0)))
```

```python
import jax
import jax.numpy as jnp
from jax import lax
from jax.experimental import pallas as pl
from jax.experimental.pallas import tpu as pltpu
from jax.sharding import PartitionSpec as P

HD = 128
EPS = 1e-06
F32 = jnp.float32
BF16 = jnp.bfloat16
MESH = pl.DeviceIdType.MESH


def dot(a, b, ca, cb):
    return lax.dot_general(a, b, (((ca,), (cb,)), ((), ())), preferred_element_type=F32)


def make_kernel(tok, feat, nc, ndp):
    heads = feat // HD
    per = heads // nc
    wid = per * HD

    def kernel(
        q_h, k_h, v_h, g_h, d_h,
        out_h, qg_h, kg_h, vg_h, gg_o,
        q_v, k_v, v_v, d_v, gain, out_v, qg_v, kg_v, vg_v,
        mix, acc, aw, ssq, cdt,
        s1, r1, p1, l1, s2, r2, p2, l2,
        gs, g1, g2s, g2, g3s, g3,
        in_sem, gain_sem, o_sem,
        s1_s, s1_r, p1_s, p1_r, s2_s, s2_r, p2_s, p2_r,
        g1_s, g1_r, g2_s, g2_r, g3_s, g3_r,
    ):
        me = lax.axis_index("context")
        row = lax.axis_index("dp")

        def cols(o):
            return pl.ds(pl.multiple_of(o * wid, wid), wid)

        def hcols(h):
            return pl.ds(pl.multiple_of(h * HD, HD), HD)

        def nxt(i):
            return lax.rem(me + 1 + i, nc)

        def load(src, dst, which, i):
            o = nxt(i)
            return pltpu.make_async_copy(src.at[:, cols(o)], dst.at[:, cols(o)], in_sem.at[which, i])

        def each(n, f):
            def body(i, carry):
                f(i)
                return carry

            lax.fori_loop(0, n, body, 0)

        def start_kv(i):
            load(k_h, k_v, 0, i).start()
            load(v_h, v_v, 1, i).start()

        def start_qd(i):
            load(q_h, q_v, 2, i).start()

        def start_d(i):
            load(d_h, d_v, 3, i).start()

        each(nc, start_kv)
        each(nc, start_qd)
        each(nc, start_d)
        gain_copy = pltpu.make_async_copy(g_h, gain, gain_sem)
        gain_copy.start()

        barrier = pltpu.get_barrier_semaphore()

        def greet_c(i):
            pl.semaphore_signal(barrier, inc=1, device_id={"context": lax.rem(me + 1 + i, nc)}, device_id_type=MESH)

        def greet_d(i):
            pl.semaphore_signal(barrier, inc=1, device_id={"dp": lax.rem(row + 1 + i, ndp)}, device_id_type=MESH)

        each(nc - 1, greet_c)
        each(ndp - 1, greet_d)
        pl.semaphore_wait(barrier, nc - 1 + ndp - 1)

        def ctx_copy(src, dst, ssem, rsem, i):
            to = lax.rem(me + 1 + i, nc)
            return pltpu.make_async_remote_copy(
                src_ref=src, dst_ref=dst.at[me], send_sem=ssem.at[i], recv_sem=rsem.at[i],
                device_id={"context": to}, device_id_type=MESH,
            )

        def dp_copy(src, dst, ssem, rsem, i):
            to = lax.rem(row + 1 + i, ndp)
            return pltpu.make_async_remote_copy(
                src_ref=src, dst_ref=dst.at[row], send_sem=ssem.at[i], recv_sem=rsem.at[i],
                device_id={"dp": to}, device_id_type=MESH,
            )

        def state_of(a, b, o, buf):
            for j in range(per):
                c = hcols(o * per + j)
                buf[o, j] = dot(a[:, c], b[:, c], 0, 0).astype(BF16)

        def step1(i):
            o = nxt(i)
            load(k_h, k_v, 0, i).wait()
            load(v_h, v_v, 1, i).wait()
            state_of(k_v, v_v, o, s1)

        def send1(i):
            ctx_copy(s1.at[nxt(i)], r1, s1_s, s1_r, i).start()

        def one1(i):
            step1(i)
            send1(i)

        each(nc - 1, one1)
        step1(nc - 1)
        r1[me] = s1[me]

        rows_i = lax.broadcasted_iota(jnp.int32, (tok, tok), 0)
        cols_i = lax.broadcasted_iota(jnp.int32, (tok, tok), 1)

        def inner(i):
            o = nxt(i)
            load(q_h, q_v, 2, i).wait()
            for j in range(per):
                h = o * per + j
                c = hcols(h)
                s = dot(q_v[:, c], k_v[:, c], 1, 1)
                a = jnp.where(rows_i >= cols_i, s, 0.0).astype(BF16)
                aw[h] = a
                mix[:, c] = dot(a, v_v[:, c], 1, 0)

        half = nc // 2
        each(half, inner)

        def scan(r, p, backward):
            def rows16(t, carry):
                rr = pl.ds(pl.multiple_of(t * 16, 16), 16)
                run = jnp.zeros((per, 16, HD), F32)
                for c in range(nc):
                    b = nc - 1 - c if backward else c
                    p[b, :, rr, :] = run.astype(BF16)
                    run = run + r[b, :, rr, :].astype(F32)
                return carry

            lax.fori_loop(0, HD // 16, rows16, 0)

        def wait_r1(i):
            ctx_copy(s1.at[nxt(i)], r1, s1_s, s1_r, i).wait_recv()

        each(nc - 1, wait_r1)
        scan(r1, p1, False)

        def back1(i):
            return ctx_copy(p1.at[nxt(i)], l1, p1_s, p1_r, i)

        each(nc - 1, lambda i: back1(i).start())
        l1[me] = p1[me]

        each(nc - half, lambda i: inner(i + half))
        gain_copy.wait()

        ssq[...] = jnp.zeros_like(ssq)
        cdt[...] = jnp.zeros_like(cdt)

        def mixed(i):
            o = nxt(i)
            load(d_h, d_v, 3, i).wait()
            for j in range(per):
                h = o * per + j
                c = hcols(h)
                m = mix[:, c] + dot(q_v[:, c], l1[o, j], 1, 0)
                mix[:, c] = m
                ssq[...] += m * m
                cdt[...] += (gain[:, c] * d_v[:, c].astype(F32)) * m

        mixed(nc - 1)

        def mixed_next(i):
            back1(nc - 2 - i).wait_recv()
            mixed(i)

        each(nc - 1, mixed_next)

        inv = lax.rsqrt(jnp.sum(ssq[...], 1, keepdims=True) / feat + EPS)
        coef = inv * inv * inv * (jnp.sum(cdt[...], 1, keepdims=True) / feat)

        def post(i):
            o = nxt(i)
            for j in range(per):
                h = o * per + j
                c = hcols(h)
                m = mix[:, c]
                dy = d_v[:, c].astype(F32)
                g = gain[:, c]
                n = m * inv
                out_v[:, c] = (n * g).astype(BF16)
                gs[:, c] = jnp.sum((dy * n).reshape(tok // 8, 8, HD), 0)
                d_v[:, c] = (inv * (g * dy) - m * coef).astype(BF16)
            pltpu.make_async_copy(out_v.at[:, cols(o)], out_h.at[:, cols(o)], o_sem.at[0]).start()
            state_of(q_v, d_v, o, s2)

        def gsend(i):
            return ctx_copy(gs.at[:, cols(nxt(i))], g1, g1_s, g1_r, i)

        def send2(i):
            return ctx_copy(s2.at[nxt(i)], r2, s2_s, s2_r, i)

        def one2(i):
            post(i)
            send2(i).start()

        each(nc - 1, one2)
        post(nc - 1)
        each(nc - 1, lambda i: gsend(i).start())
        r2[me] = s2[me]
        g1[me] = gs[:, cols(me)]

        def grads(i):
            o = nxt(i)
            for j in range(per):
                h = o * per + j
                c = hcols(h)
                dm = d_v[:, c]
                s = dot(dm, v_v[:, c], 1, 1)
                dw = jnp.where(rows_i >= cols_i, s, 0.0).astype(BF16)
                qg = dot(dw, k_v[:, c], 1, 0) + dot(dm, l1[o, j], 1, 1)
                qg_v[:, c] = qg.astype(BF16)
                mix[:, c] = dot(dw, q_v[:, c], 0, 0)
                acc[:, c] = dot(aw[h], dm, 0, 0)
            pltpu.make_async_copy(qg_v.at[:, cols(o)], qg_h.at[:, cols(o)], o_sem.at[1]).start()

        each(half, grads)

        each(nc - 1, lambda i: send2(i).wait_recv())
        scan(r2, p2, True)

        def back2(i):
            return ctx_copy(p2.at[nxt(i)], l2, p2_s, p2_r, i)

        each(nc - 1, lambda i: back2(i).start())
        l2[me] = p2[me]

        each(nc - 1, lambda i: gsend(i).wait_recv())
        part = g1[0]
        for c in range(1, nc):
            part = part + g1[c]
        g2s[...] = part
        g2[row] = part
        gdp = lambda i: dp_copy(g2s, g2, g2_s, g2_r, i)
        each(ndp - 1, lambda i: gdp(i).start())

        each(nc - half, lambda i: grads(i + half))

        each(ndp - 1, lambda i: gdp(i).wait_recv())
        total = g2[0]
        for c in range(1, ndp):
            total = total + g2[c]
        total = jnp.broadcast_to(jnp.sum(total, 0, keepdims=True), (8, wid))
        g3s[...] = total
        g3[me] = total
        gback = lambda i: ctx_copy(g3s, g3, g3_s, g3_r, i)
        each(nc - 1, lambda i: gback(i).start())

        def final(i):
            o = nxt(i)
            for j in range(per):
                h = o * per + j
                c = hcols(h)
                lb = l2[o, j]
                kg_v[:, c] = (mix[:, c] + dot(v_v[:, c], lb, 1, 1)).astype(BF16)
                vg_v[:, c] = (acc[:, c] + dot(k_v[:, c], lb, 1, 0)).astype(BF16)
            pltpu.make_async_copy(kg_v.at[:, cols(o)], kg_h.at[:, cols(o)], o_sem.at[2]).start()
            pltpu.make_async_copy(vg_v.at[:, cols(o)], vg_h.at[:, cols(o)], o_sem.at[3]).start()

        final(nc - 1)

        def final_next(i):
            back2(nc - 2 - i).wait_recv()
            final(i)

        each(nc - 1, final_next)

        each(nc - 1, lambda i: gback(i).wait_recv())
        for c in range(nc):
            gg_o[:, c * wid : (c + 1) * wid] = g3[c]

        def drain(i):
            ctx_copy(s1.at[nxt(i)], r1, s1_s, s1_r, i).wait_send()
            back1(i).wait_send()
            send2(i).wait_send()
            back2(i).wait_send()
            gsend(i).wait_send()
            gback(i).wait_send()

        each(nc - 1, drain)
        each(ndp - 1, lambda i: gdp(i).wait_send())
        pltpu.make_async_copy(out_v, out_h, o_sem.at[0]).wait()
        pltpu.make_async_copy(qg_v, qg_h, o_sem.at[1]).wait()
        pltpu.make_async_copy(kg_v, kg_h, o_sem.at[2]).wait()
        pltpu.make_async_copy(vg_v, vg_h, o_sem.at[3]).wait()

    big = jax.ShapeDtypeStruct((tok, feat), BF16)
    bufb = pltpu.VMEM((tok, feat), BF16)
    buff = pltpu.VMEM((tok, feat), F32)
    state = pltpu.VMEM((nc, per, HD, HD), BF16)
    csem = pltpu.SemaphoreType.DMA((nc - 1,))
    dsem = pltpu.SemaphoreType.DMA((ndp - 1,))
    anyspec = pl.BlockSpec(memory_space=pl.ANY)
    return pl.pallas_call(
        kernel,
        out_shape=(big, big, big, big, jax.ShapeDtypeStruct((8, feat), F32)),
        in_specs=[anyspec] * 5,
        out_specs=[anyspec] * 4 + [pl.BlockSpec(memory_space=pltpu.VMEM)],
        scratch_shapes=[
            bufb, bufb, bufb, bufb, pltpu.VMEM((1, feat), F32), bufb, bufb, bufb, bufb,
            buff, buff, pltpu.VMEM((heads, tok, tok), BF16),
            pltpu.VMEM((tok, HD), F32), pltpu.VMEM((tok, HD), F32),
            state, state, state, state, state, state, state, state,
            pltpu.VMEM((8, feat), F32), pltpu.VMEM((nc, 8, wid), F32),
            pltpu.VMEM((8, wid), F32), pltpu.VMEM((ndp, 8, wid), F32),
            pltpu.VMEM((8, wid), F32), pltpu.VMEM((nc, 8, wid), F32),
            pltpu.SemaphoreType.DMA((4, nc)), pltpu.SemaphoreType.DMA, pltpu.SemaphoreType.DMA((4,)),
            csem, csem, csem, csem, csem, csem, csem, csem,
            csem, csem, dsem, dsem, csem, csem,
        ],
        compiler_params=pltpu.CompilerParams(
            collective_id=0, has_side_effects=True, vmem_limit_bytes=67043328
        ),
        name="layer",
    )


def solution(mesh):
    nc, ndp = mesh.shape["context"], mesh.shape["dp"]

    def shards(queries, keys, values, gain, out_grad):
        tok, feat = queries.shape[1:]
        call = make_kernel(tok, feat, nc, ndp)
        out, qg, kg, vg, gg = call(queries[0], keys[0], values[0], gain[None], out_grad[0])
        return out[None], qg[None], kg[None], vg[None], gg[0]

    spec = P("dp", "context", None)
    return jax.shard_map(
        shards, mesh=mesh, in_specs=(spec, spec, spec, P(), spec),
        out_specs=(spec, spec, spec, spec, P()), check_vma=False,
    )
```

```python
import jax
import jax.numpy as jnp
from jax import lax
from jax.experimental import pallas as pl
from jax.experimental.pallas import tpu as pltpu
from jax.sharding import PartitionSpec as P

HD = 128
EPS = 1e-06
NY = 4
F32 = jnp.float32
BF16 = jnp.bfloat16
MESH = pl.DeviceIdType.MESH

FAR_FIRST = sorted(
    ((dz, dy) for dz in range(4) for dy in range(4) if dz or dy),
    key=lambda d: -(min(d[0], 4 - d[0]) + min(d[1], 4 - d[1])),
)


def dot(a, b, ca, cb):
    return lax.dot_general(a, b, (((ca,), (cb,)), ((), ())), preferred_element_type=F32)


def pick(i, values):
    if isinstance(i, int):
        return values[i]
    out = 0
    for k, v in enumerate(values):
        if v:
            out = out + jnp.where(i == k, v, 0)
    return out


def each(n, f, start=0, unroll=1):
    def body(i, carry):
        f(i)
        return carry

    lax.fori_loop(start, n, body, 0, unroll=unroll)


def hcols(h):
    return pl.ds(pl.multiple_of(h * HD, HD), HD)


def make_layer(tok, feat, nc, ndp):
    heads = feat // HD
    per = heads // nc
    wid = per * HD
    nz = nc // NY
    steps = FAR_FIRST + [(0, 0)]

    def kernel(
        q_h, k_h, v_h, g_h, d_h,
        out_v, qg_v, mix, acc, k_v, v_v, l2, gg,
        q_v, d_v, gain, aw, ssq, cdt,
        s1, r1, p1, l1, s2, r2, p2,
        gs, g1, g2s, g2, g3s, g3,
        in_sem, gain_sem,
        s1_s, s1_r, p1_s, p1_r, s2_s, s2_r, p2_s, p2_r,
        g1_s, g1_r, g2_s, g2_r, g3_s, g3_r,
    ):
        me = lax.axis_index("context")
        row = lax.axis_index("dp")
        mz, my = me // NY, lax.rem(me, NY)
        others = range(nc - 1)

        def cols(o):
            return pl.ds(pl.multiple_of(o * wid, wid), wid)

        def dest(i):
            dz, dy = pick(i, [s[0] for s in steps]), pick(i, [s[1] for s in steps])
            return lax.rem(mz + dz, nz) * NY + lax.rem(my + dy, NY)

        def source(i):
            dz, dy = pick(i, [(nz - s[0]) % nz for s in steps]), pick(i, [(NY - s[1]) % NY for s in steps])
            return lax.rem(mz + dz, nz) * NY + lax.rem(my + dy, NY)

        def load(src, dst, which, i):
            o = dest(i)
            return pltpu.make_async_copy(src.at[:, cols(o)], dst.at[:, cols(o)], in_sem.at[which, i])

        def start_kv(i):
            load(k_h, k_v, 0, i).start()
            load(v_h, v_v, 1, i).start()

        each(nc, start_kv)
        each(nc, lambda i: load(q_h, q_v, 2, i).start())
        each(nc, lambda i: load(d_h, d_v, 3, i).start())
        gain_copy = pltpu.make_async_copy(g_h, gain, gain_sem)
        gain_copy.start()

        barrier = pltpu.get_barrier_semaphore()

        def greet_c(i):
            pl.semaphore_signal(barrier, inc=1, device_id={"context": lax.rem(me + 1 + i, nc)}, device_id_type=MESH)

        def greet_d(i):
            pl.semaphore_signal(barrier, inc=1, device_id={"dp": lax.rem(row + 1 + i, ndp)}, device_id_type=MESH)

        each(nc - 1, greet_c)
        each(ndp - 1, greet_d)
        pl.semaphore_wait(barrier, nc - 1 + ndp - 1)

        def head_copy(src, dst, ssem, rsem, i, j):
            to = dest(i)
            return pltpu.make_async_remote_copy(
                src_ref=src.at[to, j], dst_ref=dst.at[me, j], send_sem=ssem.at[j, i], recv_sem=rsem.at[j, i],
                device_id={"context": to}, device_id_type=MESH,
            )

        def ctx_copy(src, dst, ssem, rsem, i):
            return pltpu.make_async_remote_copy(
                src_ref=src, dst_ref=dst.at[me], send_sem=ssem.at[i], recv_sem=rsem.at[i],
                device_id={"context": dest(i)}, device_id_type=MESH,
            )

        def dp_copy(src, dst, ssem, rsem, i):
            return pltpu.make_async_remote_copy(
                src_ref=src, dst_ref=dst.at[row], send_sem=ssem.at[i], recv_sem=rsem.at[i],
                device_id={"dp": lax.rem(row + 1 + i, ndp)}, device_id_type=MESH,
            )

        send1 = lambda i, j: head_copy(s1, r1, s1_s, s1_r, i, j)
        back1 = lambda i, j: head_copy(p1, l1, p1_s, p1_r, i, j)
        send2 = lambda i, j: head_copy(s2, r2, s2_s, s2_r, i, j)
        back2 = lambda i, j: head_copy(p2, l2, p2_s, p2_r, i, j)

        def state_of(a, b, o, j, buf):
            c = hcols(o * per + j)
            buf[o, j] = dot(a[:, c], b[:, c], 0, 0).astype(BF16)

        for j in range(per):
            def state1(i, j=j):
                if j == 0:
                    load(k_h, k_v, 0, i).wait()
                    load(v_h, v_v, 1, i).wait()
                state_of(k_v, v_v, dest(i), j, s1)

            def one1(i, j=j):
                state1(i)
                send1(i, j).start()

            each(nc - 1, one1, unroll=3)
            state1(nc - 1)
            r1[me, j] = s1[me, j]

        rows_i = lax.broadcasted_iota(jnp.int32, (tok, tok), 0)
        cols_i = lax.broadcasted_iota(jnp.int32, (tok, tok), 1)

        def inner(i):
            o = dest(i)
            load(q_h, q_v, 2, i).wait()
            for j in range(per):
                h = o * per + j
                c = hcols(h)
                s = dot(q_v[:, c], k_v[:, c], 1, 1)
                a = jnp.where(rows_i >= cols_i, s, 0.0).astype(BF16)
                aw[h] = a
                mix[:, c] = dot(a, v_v[:, c], 1, 0)

        def scan(r, p, j, backward):
            def rows16(t):
                rr = pl.ds(pl.multiple_of(t * 16, 16), 16)
                run = jnp.zeros((16, HD), F32)
                for c in range(nc):
                    b = nc - 1 - c if backward else c
                    p[b, j, rr, :] = run.astype(BF16)
                    run = run + r[b, j, rr, :].astype(F32)

            each(HD // 16, rows16, unroll=2)

        def turn(send, back, r, p, l, j, backward):
            for i in others:
                send(i, j).wait_recv()
            scan(r, p, j, backward)
            for i in others:
                back(i, j).start()
            l[me, j] = p[me, j]

        n1 = 11
        each(n1, inner)
        turn(send1, back1, r1, p1, l1, 0, False)
        each(nc, inner, n1)
        turn(send1, back1, r1, p1, l1, 1, False)
        gain_copy.wait()
        each(nc, lambda i: load(d_h, d_v, 3, i).wait())

        ssq[...] = jnp.zeros_like(ssq)
        cdt[...] = jnp.zeros_like(cdt)

        def mixed(o, j):
            c = hcols(o * per + j)
            m = mix[:, c] + dot(q_v[:, c], l1[o, j], 1, 0)
            mix[:, c] = m
            ssq[...] += m * m
            cdt[...] += (gain[:, c] * d_v[:, c].astype(F32)) * m

        for j in range(per):
            mixed(me, j)

            def mixed_next(i, j=j):
                back1(i, j).wait_recv()
                mixed(source(i), j)

            each(nc - 1, mixed_next)

        inv = lax.rsqrt(jnp.sum(ssq[...], 1, keepdims=True) / feat + EPS)
        coef = inv * inv * inv * (jnp.sum(cdt[...], 1, keepdims=True) / feat)

        def post(i):
            o = dest(i)
            for j in range(per):
                c = hcols(o * per + j)
                m = mix[:, c]
                dy = d_v[:, c].astype(F32)
                g = gain[:, c]
                n = m * inv
                out_v[:, c] = (n * g).astype(BF16)
                gs[:, c] = jnp.sum((dy * n).reshape(tok // 8, 8, HD), 0)
                d_v[:, c] = (inv * (g * dy) - m * coef).astype(BF16)
            state_of(q_v, d_v, o, 0, s2)

        gsend = lambda i: ctx_copy(gs.at[:, cols(dest(i))], g1, g1_s, g1_r, i)

        def one2(i):
            post(i)
            send2(i, 0).start()

        each(nc - 1, one2)
        post(nc - 1)
        for i in others:
            gsend(i).start()
        r2[me, 0] = s2[me, 0]
        g1[me] = gs[:, cols(me)]

        for j in range(1, per):
            def two2(i, j=j):
                state_of(q_v, d_v, dest(i), j, s2)
                send2(i, j).start()

            each(nc - 1, two2, unroll=3)
            state_of(q_v, d_v, me, j, s2)
            r2[me, j] = s2[me, j]

        def grads(i):
            o = dest(i)
            for j in range(per):
                h = o * per + j
                c = hcols(h)
                dm = d_v[:, c]
                s = dot(dm, v_v[:, c], 1, 1)
                dw = jnp.where(rows_i >= cols_i, s, 0.0).astype(BF16)
                qg = dot(dw, k_v[:, c], 1, 0) + dot(dm, l1[o, j], 1, 1)
                qg_v[:, c] = qg.astype(BF16)
                mix[:, c] = dot(dw, q_v[:, c], 0, 0)
                acc[:, c] = dot(aw[h], dm, 0, 0)

        m1, m2 = 3, 8
        each(m1, grads)
        turn(send2, back2, r2, p2, l2, 0, True)

        for i in others:
            gsend(i).wait_recv()
        part = g1[0]
        for c in range(1, nc):
            part = part + g1[c]
        g2s[...] = part
        g2[row] = part
        gdp = lambda i: dp_copy(g2s, g2, g2_s, g2_r, i)
        for i in range(ndp - 1):
            gdp(i).start()

        each(m2, grads, m1)

        for i in range(ndp - 1):
            gdp(i).wait_recv()
        total = g2[0]
        for c in range(1, ndp):
            total = total + g2[c]
        total = jnp.broadcast_to(jnp.sum(total, 0, keepdims=True), (8, wid))
        g3s[...] = total
        g3[me] = total
        gback = lambda i: ctx_copy(g3s, g3, g3_s, g3_r, i)
        for i in others:
            gback(i).start()

        turn(send2, back2, r2, p2, l2, 1, True)
        each(nc, grads, m2)

        for i in others:
            gback(i).wait_recv()
        for c in range(nc):
            gg[:, c * wid : (c + 1) * wid] = g3[c]

        for i in others:
            for j in range(per):
                send1(i, j).wait_send()
                back1(i, j).wait_send()
                send2(i, j).wait_send()
                back2(i, j).wait_send()
            gsend(i).wait_send()
            gback(i).wait_send()
        for i in range(ndp - 1):
            gdp(i).wait_send()
        for j in range(per):
            for i in others:
                back2(i, j).wait_recv()

    bufb = pltpu.VMEM((tok, feat), BF16)
    buff = pltpu.VMEM((tok, feat), F32)
    state = pltpu.VMEM((nc, per, HD, HD), BF16)
    hsem = pltpu.SemaphoreType.DMA((per, nc - 1))
    csem = pltpu.SemaphoreType.DMA((nc - 1,))
    dsem = pltpu.SemaphoreType.DMA((ndp - 1,))
    part = pltpu.VMEM((8, wid), F32)
    return pl.pallas_call(
        kernel,
        out_shape=(bufb, bufb, buff, buff, bufb, bufb, state, pltpu.VMEM((8, feat), F32)),
        in_specs=[pl.BlockSpec(memory_space=pltpu.MemorySpace.HBM)] * 5,
        out_specs=[pl.BlockSpec(memory_space=pltpu.VMEM)] * 8,
        scratch_shapes=[
            bufb, bufb, pltpu.VMEM((1, feat), F32), pltpu.VMEM((heads, tok, tok), BF16),
            pltpu.VMEM((tok, HD), F32), pltpu.VMEM((tok, HD), F32),
            state, state, state, state, state, state, state,
            pltpu.VMEM((8, feat), F32), pltpu.VMEM((nc, 8, wid), F32),
            part, pltpu.VMEM((ndp, 8, wid), F32), part, pltpu.VMEM((nc, 8, wid), F32),
            pltpu.SemaphoreType.DMA((4, nc)), pltpu.SemaphoreType.DMA,
            hsem, hsem, hsem, hsem, hsem, hsem, hsem, hsem,
            csem, csem, dsem, dsem, csem, csem,
        ],
        compiler_params=pltpu.CompilerParams(
            collective_id=0, has_side_effects=True, vmem_limit_bytes=32 * 2**20
        ),
        name="layer",
    )


def make_finish(tok, feat, nc):
    per = feat // HD // nc
    wid = per * HD

    def kernel(out_v, qg_v, mix, acc, k_v, v_v, l2, gg, out_h, qg_h, kg_h, vg_h, gg_o, kg_v, vg_v, sem):
        whole = [
            pltpu.make_async_copy(out_v, out_h, sem.at[0]),
            pltpu.make_async_copy(qg_v, qg_h, sem.at[1]),
            pltpu.make_async_copy(kg_v, kg_h, sem.at[2]),
            pltpu.make_async_copy(vg_v, vg_h, sem.at[3]),
        ]
        whole[0].start()
        whole[1].start()
        gg_o[...] = gg[0:1, :]

        def final(o):
            cc = pl.ds(pl.multiple_of(o * wid, wid), wid)
            for j in range(per):
                c = hcols(o * per + j)
                lb = l2[o, j]
                kg_v[:, c] = (mix[:, c] + dot(v_v[:, c], lb, 1, 1)).astype(BF16)
                vg_v[:, c] = (acc[:, c] + dot(k_v[:, c], lb, 1, 0)).astype(BF16)
            pltpu.make_async_copy(kg_v.at[:, cc], kg_h.at[:, cc], sem.at[2]).start()
            pltpu.make_async_copy(vg_v.at[:, cc], vg_h.at[:, cc], sem.at[3]).start()

        each(nc, final)
        for w in whole:
            w.wait()

    big = jax.ShapeDtypeStruct((tok, feat), BF16)
    bufb = pltpu.VMEM((tok, feat), BF16)
    vm = pl.BlockSpec(memory_space=pltpu.VMEM)
    return pl.pallas_call(
        kernel,
        out_shape=(big, big, big, big, jax.ShapeDtypeStruct((1, feat), F32)),
        in_specs=[vm] * 8,
        out_specs=[pl.BlockSpec(memory_space=pltpu.MemorySpace.HBM)] * 4 + [vm],
        scratch_shapes=[bufb, bufb, pltpu.SemaphoreType.DMA((4,))],
        compiler_params=pltpu.CompilerParams(vmem_limit_bytes=12 * 2**20),
        name="finish",
    )


def solution(mesh):
    nc, ndp = mesh.shape["context"], mesh.shape["dp"]

    def shards(queries, keys, values, gain, out_grad):
        tok, feat = queries.shape[1:]
        held = make_layer(tok, feat, nc, ndp)(queries[0], keys[0], values[0], gain[None], out_grad[0])
        out, qg, kg, vg, gg = make_finish(tok, feat, nc)(*held)
        return out[None], qg[None], kg[None], vg[None], gg[0]

    spec = P("dp", "context", None)
    return jax.shard_map(
        shards, mesh=mesh, in_specs=(spec, spec, spec, P(), spec),
        out_specs=(spec, spec, spec, spec, P()), check_vma=False,
    )
```

```python
import jax
import jax.numpy as jnp
from jax import lax
from jax.experimental import pallas as pl
from jax.experimental.pallas import tpu as pltpu
from jax.sharding import PartitionSpec as P

HD = 128
EPS = 1e-06
NY = 4
F32 = jnp.float32
BF16 = jnp.bfloat16
MESH = pl.DeviceIdType.MESH

FAR_FIRST = sorted(
    ((dz, dy) for dz in range(4) for dy in range(4) if dz or dy),
    key=lambda d: -(min(d[0], 4 - d[0]) + min(d[1], 4 - d[1])),
)


def dot(a, b, ca, cb):
    return lax.dot_general(a, b, (((ca,), (cb,)), ((), ())), preferred_element_type=F32)


def pick(i, values):
    if isinstance(i, int):
        return values[i]
    out = 0
    for k, v in enumerate(values):
        if v:
            out = out + jnp.where(i == k, v, 0)
    return out


def each(n, f, start=0, unroll=1):
    def body(i, carry):
        f(i)
        return carry

    lax.fori_loop(start, n, body, 0, unroll=unroll)


def hcols(h):
    return pl.ds(pl.multiple_of(h * HD, HD), HD)


def make_layer(tok, feat, nc, ndp):
    heads = feat // HD
    per = heads // nc
    wid = per * HD
    nz = nc // NY
    top = min(256, tok)
    low = tok - top
    nload = 8
    lw = feat // nload
    steps = FAR_FIRST + [(0, 0)]

    def kernel(
        q_h, k_h, v_h, g_h, d_h,
        out_v, qg_v, mix, acc, k_v, v_v, l2, gg,
        q_v, d_v, gain, aw0, aw1, ssq, cdt,
        s1, r1, p1, l1, s2, r2, p2,
        gs, g1, g2s, g2, g3s, g3,
        kv_sem, q_sem, d_sem, gain_sem,
        s1_s, s1_r, p1_s, p1_ra, p1_rb, s2_s, s2_r, p2_s, p2_r,
        g1_s, g1_r, g2_s, g2_r, g3_s, g3_r,
    ):
        me = lax.axis_index("context")
        row = lax.axis_index("dp")
        mz, my = me // NY, lax.rem(me, NY)
        others = range(nc - 1)

        def cols(o):
            return pl.ds(pl.multiple_of(o * wid, wid), wid)

        def dest(i):
            dz, dy = pick(i, [s[0] for s in steps]), pick(i, [s[1] for s in steps])
            return lax.rem(mz + dz, nz) * NY + lax.rem(my + dy, NY)

        def source(i):
            dz, dy = pick(i, [(nz - s[0]) % nz for s in steps]), pick(i, [(NY - s[1]) % NY for s in steps])
            return lax.rem(mz + dz, nz) * NY + lax.rem(my + dy, NY)

        barrier = pltpu.get_barrier_semaphore()
        for i in others:
            pl.semaphore_signal(barrier, inc=1, device_id={"context": dest(i)}, device_id_type=MESH)
        for i in range(ndp - 1):
            pl.semaphore_signal(barrier, inc=1, device_id={"dp": lax.rem(row + 1 + i, ndp)}, device_id_type=MESH)

        def kv_load(src, dst, which, i):
            c = slice(i * lw, (i + 1) * lw)
            return pltpu.make_async_copy(src.at[:, c], dst.at[:, c], kv_sem.at[which, i])

        for i in range(nload):
            kv_load(k_h, k_v, 0, i).start()
            kv_load(v_h, v_v, 1, i).start()
        q_copy = pltpu.make_async_copy(q_h, q_v, q_sem)
        d_copy = pltpu.make_async_copy(d_h, d_v, d_sem)
        gain_copy = pltpu.make_async_copy(g_h, gain, gain_sem)
        q_copy.start()
        d_copy.start()
        gain_copy.start()

        def pair_state(a, b, o, buf):
            c = cols(o)
            s = dot(a[:, c], b[:, c], 0, 0)
            for j in range(per):
                buf[o, j] = s[j * HD : (j + 1) * HD, j * HD : (j + 1) * HD].astype(BF16)

        def clear(i):
            for j in range(per):
                for k in range(per):
                    if j != k:
                        z = jnp.zeros((HD, HD), BF16)
                        l1[i, j * HD : (j + 1) * HD, k * HD : (k + 1) * HD] = z
                        l2[i, j * HD : (j + 1) * HD, k * HD : (k + 1) * HD] = z

        each(nc, clear)

        for i in range(nload):
            kv_load(k_h, k_v, 0, i).wait()
            kv_load(v_h, v_v, 1, i).wait()
            for o in range(i * nc // nload, (i + 1) * nc // nload):
                pair_state(k_v, v_v, o, s1)

        pl.semaphore_wait(barrier, nc - 1 + ndp - 1)

        def ctx_copy(src, dst, ssem, rsem, i):
            return pltpu.make_async_remote_copy(
                src_ref=src, dst_ref=dst, send_sem=ssem, recv_sem=rsem,
                device_id={"context": dest(i)}, device_id_type=MESH,
            )

        def out_copy(src, dst, ssem, rsem, i, j):
            return ctx_copy(src.at[dest(i), j], dst.at[me, j], ssem, rsem.at[j], i)

        def back_copy(src, dst, ssem, rsem, i, j):
            place = dst.at[me, j * HD : (j + 1) * HD, j * HD : (j + 1) * HD]
            return ctx_copy(src.at[dest(i), j], place, ssem, rsem, i)

        def take(src, dst, sem):
            pltpu.make_async_copy(src, dst, sem).wait()

        def own_state(p, l, j):
            l[me, j * HD : (j + 1) * HD, j * HD : (j + 1) * HD] = p[me, j]

        def scan(r, p, j, backward):
            def rows32(t):
                rr = pl.ds(pl.multiple_of(t * 32, 32), 32)
                run = jnp.zeros((32, HD), F32)
                for c in range(nc):
                    b = nc - 1 - c if backward else c
                    p[b, j, rr, :] = run.astype(BF16)
                    run = run + r[b, j, rr, :].astype(F32)

            each(HD // 32, rows32, unroll=2)

        def back1(i, j):
            return back_copy(p1, l1, p1_s, p1_ra if j == 0 else p1_rb.at[j - 1, i], i, j)

        def back2(i, j):
            return back_copy(p2, l2, p2_s, p2_r, i, j)

        def turn(s, r, rsem, back, p, l, j, backward):
            take(s.at[0 : nc - 1, j], r.at[0 : nc - 1, j], rsem.at[j])
            scan(r, p, j, backward)
            for i in others:
                back(i, j).start()
            own_state(p, l, j)

        for j in range(per):
            for i in others:
                out_copy(s1, r1, s1_s, s1_r, i, j).start()
            r1[me, j] = s1[me, j]

        keep0 = lax.broadcasted_iota(jnp.int32, (top, top), 0) >= lax.broadcasted_iota(jnp.int32, (top, top), 1)
        keep1 = lax.broadcasted_iota(jnp.int32, (low, tok), 0) + top >= lax.broadcasted_iota(jnp.int32, (low, tok), 1)

        def weights(a, b):
            w0 = jnp.where(keep0, dot(a[:top], b[:top], 1, 1), 0.0).astype(BF16)
            w1 = jnp.where(keep1, dot(a[top:], b, 1, 1), 0.0).astype(BF16)
            return w0, w1

        def inner(o):
            for j in range(per):
                h = o * per + j
                c = hcols(h)
                v = v_v[:, c]
                w0, w1 = weights(q_v[:, c], k_v[:, c])
                aw0[h] = w0
                aw1[h] = w1
                mix[:top, c] = dot(w0, v[:top], 1, 0)
                mix[top:, c] = dot(w1, v, 1, 0)

        q_copy.wait()
        n1 = 13
        each(n1, inner)
        turn(s1, r1, s1_r, back1, p1, l1, 0, False)
        each(nc, inner, n1)
        for j in range(1, per):
            turn(s1, r1, s1_r, back1, p1, l1, j, False)
        gain_copy.wait()
        d_copy.wait()

        ssq[...] = jnp.zeros_like(ssq)
        cdt[...] = jnp.zeros_like(cdt)

        def fold(x):
            return sum(x[:, j * HD : (j + 1) * HD] for j in range(per))

        def mixed(o):
            c = cols(o)
            m = mix[:, c] + dot(q_v[:, c], l1[o], 1, 0)
            mix[:, c] = m
            ssq[...] += fold(m * m)
            cdt[...] += fold((gain[:, c] * d_v[:, c].astype(F32)) * m)

        take(p1.at[0 : nc - 1, 0], p1.at[0 : nc - 1, 0], p1_ra)
        mixed(me)

        def mixed_next(i):
            for j in range(1, per):
                back1(i, j).wait_recv()
            mixed(source(i))

        each(nc - 1, mixed_next)

        inv = lax.rsqrt(jnp.sum(ssq[...], 1, keepdims=True) / feat + EPS)
        coef = inv * inv * inv * (jnp.sum(cdt[...], 1, keepdims=True) / feat)

        def post(i):
            o = dest(i)
            c = cols(o)
            m = mix[:, c]
            dy = d_v[:, c].astype(F32)
            g = gain[:, c]
            n = m * inv
            out_v[:, c] = (n * g).astype(BF16)
            gs[o] = jnp.sum(dy * n, 0, keepdims=True)
            d_v[:, c] = (inv * (g * dy) - m * coef).astype(BF16)
            pair_state(q_v, d_v, o, s2)

        def post_send(i):
            post(i)
            out_copy(s2, r2, s2_s, s2_r, i, 0).start()

        each(nc - 1, post_send)
        post(nc - 1)
        for i in others:
            ctx_copy(gs.at[dest(i)], g1.at[me], g1_s, g1_r, i).start()
        for j in range(1, per):
            for i in others:
                out_copy(s2, r2, s2_s, s2_r, i, j).start()
        for j in range(per):
            r2[me, j] = s2[me, j]
        g1[me] = gs[me]

        def grads(o):
            cc = cols(o)
            far = dot(d_v[:, cc], l1[o], 1, 1)
            for j in range(per):
                h = o * per + j
                c = hcols(h)
                dm, k, q = d_v[:, c], k_v[:, c], q_v[:, c]
                w0, w1 = weights(dm, v_v[:, c])
                f = far[:, j * HD : (j + 1) * HD]
                qg_v[:top, c] = (dot(w0, k[:top], 1, 0) + f[:top]).astype(BF16)
                qg_v[top:, c] = (dot(w1, k, 1, 0) + f[top:]).astype(BF16)
                t = dot(w1, q[top:], 0, 0)
                mix[:top, c] = dot(w0, q[:top], 0, 0) + t[:top]
                mix[top:, c] = t[top:]
                t = dot(aw1[h], dm[top:], 0, 0)
                acc[:top, c] = dot(aw0[h], dm[:top], 0, 0) + t[:top]
                acc[top:, c] = t[top:]

        m1, m2 = 7, 14
        each(m1, grads)
        turn(s2, r2, s2_r, back2, p2, l2, 0, True)

        take(gs.at[0 : nc - 1], g1.at[0 : nc - 1], g1_r)
        part = g1[0]
        for c in range(1, nc):
            part = part + g1[c]
        g2s[...] = part
        g2[row] = part

        for i in range(ndp - 1):
            pltpu.make_async_remote_copy(
                src_ref=g2s, dst_ref=g2.at[row], send_sem=g2_s, recv_sem=g2_r,
                device_id={"dp": lax.rem(row + 1 + i, ndp)}, device_id_type=MESH,
            ).start()

        each(m2, grads, m1)

        take(g2.at[0 : ndp - 1], g2.at[0 : ndp - 1], g2_r)
        total = g2[0]
        for c in range(1, ndp):
            total = total + g2[c]
        g3s[...] = total
        g3[me] = total
        for i in others:
            ctx_copy(g3s, g3.at[me], g3_s, g3_r, i).start()

        for j in range(1, per):
            turn(s2, r2, s2_r, back2, p2, l2, j, True)
        each(nc, grads, m2)

        take(g3.at[0 : nc - 1], g3.at[0 : nc - 1], g3_r)
        for c in range(nc):
            gg[:, c * wid : (c + 1) * wid] = g3[c]

        for p, sem in ((s1, s1_s), (p1, p1_s), (s2, s2_s), (p2, p2_s), (g1, g1_s), (g3, g3_s)):
            take(p.at[0 : nc - 1], p.at[0 : nc - 1], sem)
        take(g2.at[0 : ndp - 1], g2.at[0 : ndp - 1], g2_s)
        take(p2.at[0 : nc - 1], p2.at[0 : nc - 1], p2_r)

    bufb = pltpu.VMEM((tok, feat), BF16)
    buff = pltpu.VMEM((tok, feat), F32)
    state = pltpu.VMEM((nc, per, HD, HD), BF16)
    square = pltpu.VMEM((nc, wid, wid), BF16)
    one = pltpu.SemaphoreType.DMA
    part = pltpu.VMEM((1, wid), F32)
    parts = pltpu.VMEM((nc, 1, wid), F32)
    return pl.pallas_call(
        kernel,
        out_shape=(bufb, bufb, buff, buff, bufb, bufb, square, pltpu.VMEM((1, feat), F32)),
        in_specs=[pl.BlockSpec(memory_space=pltpu.MemorySpace.HBM)] * 5,
        out_specs=[pl.BlockSpec(memory_space=pltpu.VMEM)] * 8,
        scratch_shapes=[
            bufb, bufb, pltpu.VMEM((1, feat), F32),
            pltpu.VMEM((heads, top, top), BF16), pltpu.VMEM((heads, low, tok), BF16),
            pltpu.VMEM((tok, HD), F32), pltpu.VMEM((tok, HD), F32),
            state, state, state, square, state, state, state,
            parts, parts, part, pltpu.VMEM((ndp, 1, wid), F32), part, parts,
            one((2, nload)), one, one, one,
            one, one((per,)), one, one, one((per - 1, nc - 1)), one, one((per,)), one, one,
            one, one, one, one, one, one,
        ],
        compiler_params=pltpu.CompilerParams(
            collective_id=0, has_side_effects=True, vmem_limit_bytes=32 * 2**20
        ),
        name="layer",
    )


def make_finish(tok, feat, nc):
    per = feat // HD // nc
    wid = per * HD

    def kernel(out_v, qg_v, mix, acc, k_v, v_v, l2, gg, out_h, qg_h, kg_h, vg_h, gg_o, kg_v, vg_v, sem):
        whole = [
            pltpu.make_async_copy(out_v, out_h, sem.at[0]),
            pltpu.make_async_copy(qg_v, qg_h, sem.at[1]),
            pltpu.make_async_copy(kg_v, kg_h, sem.at[2]),
            pltpu.make_async_copy(vg_v, vg_h, sem.at[3]),
        ]
        whole[0].start()
        whole[1].start()
        gg_o[...] = gg[...]

        def final(o):
            c = pl.ds(pl.multiple_of(o * wid, wid), wid)
            kg_v[:, c] = (mix[:, c] + dot(v_v[:, c], l2[o], 1, 1)).astype(BF16)
            vg_v[:, c] = (acc[:, c] + dot(k_v[:, c], l2[o], 1, 0)).astype(BF16)
            pltpu.make_async_copy(kg_v.at[:, c], kg_h.at[:, c], sem.at[2]).start()
            pltpu.make_async_copy(vg_v.at[:, c], vg_h.at[:, c], sem.at[3]).start()

        each(nc, final)
        for w in whole:
            w.wait()

    big = jax.ShapeDtypeStruct((tok, feat), BF16)
    bufb = pltpu.VMEM((tok, feat), BF16)
    vm = pl.BlockSpec(memory_space=pltpu.VMEM)
    return pl.pallas_call(
        kernel,
        out_shape=(big, big, big, big, jax.ShapeDtypeStruct((1, feat), F32)),
        in_specs=[vm] * 8,
        out_specs=[pl.BlockSpec(memory_space=pltpu.MemorySpace.HBM)] * 4 + [vm],
        scratch_shapes=[bufb, bufb, pltpu.SemaphoreType.DMA((4,))],
        compiler_params=pltpu.CompilerParams(vmem_limit_bytes=12 * 2**20),
        name="finish",
    )


def solution(mesh):
    nc, ndp = mesh.shape["context"], mesh.shape["dp"]

    def shards(queries, keys, values, gain, out_grad):
        tok, feat = queries.shape[1:]
        held = make_layer(tok, feat, nc, ndp)(
            queries[0], keys[0], values[0],
            pltpu.with_memory_space_constraint(gain[None], pltpu.MemorySpace.HBM), out_grad[0],
        )
        out, qg, kg, vg, gg = make_finish(tok, feat, nc)(*held)
        return out[None], qg[None], kg[None], vg[None], gg[0]

    spec = P("dp", "context", None)
    return jax.shard_map(
        shards, mesh=mesh, in_specs=(spec, spec, spec, P(), spec),
        out_specs=(spec, spec, spec, spec, P()), check_vma=False,
    )
```

```python
import jax
import jax.numpy as jnp
from jax import lax
from jax.experimental import pallas as pl
from jax.experimental.pallas import tpu as pltpu
from jax.sharding import PartitionSpec as P

HD = 128
EPS = 1e-06
NY = 4
F32 = jnp.float32
BF16 = jnp.bfloat16
MESH = pl.DeviceIdType.MESH

FAR_FIRST = sorted(
    ((dz, dy) for dz in range(4) for dy in range(4) if dz or dy),
    key=lambda d: -(min(d[0], 4 - d[0]) + min(d[1], 4 - d[1])),
)


def dot(a, b, ca, cb):
    return lax.dot_general(a, b, (((ca,), (cb,)), ((), ())), preferred_element_type=F32)


def pick(i, values):
    if isinstance(i, int):
        return values[i]
    out = 0
    for k, v in enumerate(values):
        if v:
            out = out + jnp.where(i == k, v, 0)
    return out


def each(n, f, start=0, unroll=1):
    def body(i, carry):
        f(i)
        return carry

    lax.fori_loop(start, n, body, 0, unroll=unroll)


def hcols(h):
    return pl.ds(pl.multiple_of(h * HD, HD), HD)


def make_layer(tok, feat, nc, ndp):
    heads = feat // HD
    per = heads // nc
    wid = per * HD
    nz = nc // NY
    top = min(256, tok)
    low = tok - top
    nload = 8
    lw = feat // nload
    steps = FAR_FIRST + [(0, 0)]

    def kernel(
        q_h, k_h, v_h, g_h, d_h,
        out_v, qg_v, mix, acc, k_v, v_v, l2, gg,
        q_v, d_v, gain, aw0, aw1, ssq, cdt,
        s1, r1, p1, l1, s2, r2, p2,
        gs, g1, g2s, g2, g3s, g3,
        kv_sem, q_sem, d_sem, gain_sem,
        s1_s, s1_r, p1_s, p1_r, s2_s, s2_r, p2_s, p2_r,
        g1_s, g1_r, g2_s, g2_r, g3_s, g3_r,
    ):
        me = lax.axis_index("context")
        row = lax.axis_index("dp")
        mz, my = me // NY, lax.rem(me, NY)
        others = range(nc - 1)

        def cols(o):
            return pl.ds(pl.multiple_of(o * wid, wid), wid)

        def dest(i):
            dz, dy = pick(i, [s[0] for s in steps]), pick(i, [s[1] for s in steps])
            return lax.rem(mz + dz, nz) * NY + lax.rem(my + dy, NY)

        def source(i):
            dz, dy = pick(i, [(nz - s[0]) % nz for s in steps]), pick(i, [(NY - s[1]) % NY for s in steps])
            return lax.rem(mz + dz, nz) * NY + lax.rem(my + dy, NY)

        def kv_load(src, dst, which, i):
            c = slice(i * lw, (i + 1) * lw)
            return pltpu.make_async_copy(src.at[:, c], dst.at[:, c], kv_sem.at[which, i])

        def kv_start(i):
            kv_load(k_h, k_v, 0, i).start()
            kv_load(v_h, v_v, 1, i).start()

        for i in range(2):
            kv_start(i)

        barrier = pltpu.get_barrier_semaphore()
        for i in others:
            pl.semaphore_signal(barrier, inc=1, device_id={"context": dest(i)}, device_id_type=MESH)
        for i in range(ndp - 1):
            pl.semaphore_signal(barrier, inc=1, device_id={"dp": lax.rem(row + 1 + i, ndp)}, device_id_type=MESH)

        for i in range(2, nload):
            kv_start(i)
        q_copy = pltpu.make_async_copy(q_h, q_v, q_sem)
        d_copy = pltpu.make_async_copy(d_h, d_v, d_sem)
        gain_copy = pltpu.make_async_copy(g_h, gain, gain_sem)
        q_copy.start()
        d_copy.start()
        gain_copy.start()

        def pair_state(a, b, o, buf):
            c = cols(o)
            s = dot(a[:, c], b[:, c], 0, 0)
            for j in range(per):
                buf[o, j] = s[j * HD : (j + 1) * HD, j * HD : (j + 1) * HD].astype(BF16)

        def clear(i):
            for j in range(per):
                for k in range(per):
                    if j != k:
                        z = jnp.zeros((HD, HD), BF16)
                        l1[i, j * HD : (j + 1) * HD, k * HD : (k + 1) * HD] = z
                        l2[i, j * HD : (j + 1) * HD, k * HD : (k + 1) * HD] = z

        each(nc, clear)

        for i in range(nload):
            kv_load(k_h, k_v, 0, i).wait()
            kv_load(v_h, v_v, 1, i).wait()
            for o in range(i * nc // nload, (i + 1) * nc // nload):
                pair_state(k_v, v_v, o, s1)

        pl.semaphore_wait(barrier, nc - 1 + ndp - 1)

        def ctx_copy(src, dst, ssem, rsem, i):
            return pltpu.make_async_remote_copy(
                src_ref=src, dst_ref=dst, send_sem=ssem, recv_sem=rsem,
                device_id={"context": dest(i)}, device_id_type=MESH,
            )

        def out_copy(src, dst, ssem, rsem, i, j):
            return ctx_copy(src.at[dest(i), j], dst.at[me, j], ssem, rsem.at[j], i)

        def back_copy(src, dst, ssem, rsem, i, j):
            place = dst.at[me, j * HD : (j + 1) * HD, j * HD : (j + 1) * HD]
            return ctx_copy(src.at[dest(i), j], place, ssem, rsem, i)

        def take(src, dst, sem):
            pltpu.make_async_copy(src, dst, sem).wait()

        def own_state(p, l, j):
            l[me, j * HD : (j + 1) * HD, j * HD : (j + 1) * HD] = p[me, j]

        def scan(r, p, j, backward):
            def rows32(t):
                rr = pl.ds(pl.multiple_of(t * 32, 32), 32)
                run = jnp.zeros((32, HD), F32)
                for c in range(nc):
                    b = nc - 1 - c if backward else c
                    p[b, j, rr, :] = run.astype(BF16)
                    run = run + r[b, j, rr, :].astype(F32)

            each(HD // 32, rows32, unroll=2)

        def back1(i, j):
            return back_copy(p1, l1, p1_s, p1_r.at[j], i, j)

        def back2(i, j):
            return back_copy(p2, l2, p2_s, p2_r, i, j)

        def turn(s, r, rsem, back, p, l, j, backward):
            take(s.at[0 : nc - 1, j], r.at[0 : nc - 1, j], rsem.at[j])
            scan(r, p, j, backward)
            for i in others:
                back(i, j).start()
            own_state(p, l, j)

        for j in range(per):
            for i in others:
                out_copy(s1, r1, s1_s, s1_r, i, j).start()
            r1[me, j] = s1[me, j]

        keep0 = lax.broadcasted_iota(jnp.int32, (top, top), 0) >= lax.broadcasted_iota(jnp.int32, (top, top), 1)
        keep1 = lax.broadcasted_iota(jnp.int32, (low, tok), 0) + top >= lax.broadcasted_iota(jnp.int32, (low, tok), 1)

        def weights(a, b):
            w0 = jnp.where(keep0, dot(a[:top], b[:top], 1, 1), 0.0).astype(BF16)
            w1 = jnp.where(keep1, dot(a[top:], b, 1, 1), 0.0).astype(BF16)
            return w0, w1

        def inner(o):
            for j in range(per):
                h = o * per + j
                c = hcols(h)
                v = v_v[:, c]
                w0, w1 = weights(q_v[:, c], k_v[:, c])
                aw0[h] = w0
                aw1[h] = w1
                mix[:top, c] = dot(w0, v[:top], 1, 0)
                mix[top:, c] = dot(w1, v, 1, 0)

        q_copy.wait()
        n1 = 13
        each(n1, inner)
        turn(s1, r1, s1_r, back1, p1, l1, 0, False)
        each(nc, inner, n1)
        for j in range(1, per):
            turn(s1, r1, s1_r, back1, p1, l1, j, False)
        gain_copy.wait()
        d_copy.wait()

        ssq[...] = jnp.zeros_like(ssq)
        cdt[...] = jnp.zeros_like(cdt)

        group = 4

        def mixed(t, j):
            sq, cd = 0.0, 0.0
            for k in range(group):
                o = t * group + k
                c = hcols(o * per + j)
                m = mix[:, c] + dot(q_v[:, c], l1[o, j * HD : (j + 1) * HD, j * HD : (j + 1) * HD], 1, 0)
                mix[:, c] = m
                sq = sq + m * m
                cd = cd + (gain[:, c] * d_v[:, c].astype(F32)) * m
            ssq[...] += sq
            cdt[...] += cd

        for j in range(per):
            take(p1.at[0 : nc - 1, j], p1.at[0 : nc - 1, j], p1_r.at[j])
            each(nc // group, lambda t, j=j: mixed(t, j))

        inv = lax.rsqrt(jnp.sum(ssq[...], 1, keepdims=True) / feat + EPS)
        coef = inv * inv * inv * (jnp.sum(cdt[...], 1, keepdims=True) / feat)
        ssq[...] = jnp.broadcast_to(inv, ssq.shape)
        cdt[...] = jnp.broadcast_to(coef, cdt.shape)

        def post(i):
            o = dest(i)
            for j in range(per):
                c = hcols(o * per + j)
                m = mix[:, c]
                dy = d_v[:, c].astype(F32)
                g = gain[:, c]
                n = m * ssq[...]
                out_v[:, c] = (n * g).astype(BF16)
                gs[o, :, j * HD : (j + 1) * HD] = jnp.sum(dy * n, 0, keepdims=True)
                d_v[:, c] = (ssq[...] * (g * dy) - m * cdt[...]).astype(BF16)
            pair_state(q_v, d_v, o, s2)

        def post_send(i):
            post(i)
            out_copy(s2, r2, s2_s, s2_r, i, 0).start()

        each(nc - 1, post_send)
        post(nc - 1)
        for i in others:
            ctx_copy(gs.at[dest(i)], g1.at[me], g1_s, g1_r, i).start()
        for j in range(1, per):
            for i in others:
                out_copy(s2, r2, s2_s, s2_r, i, j).start()
        for j in range(per):
            r2[me, j] = s2[me, j]
        g1[me] = gs[me]

        def grads(o):
            cc = cols(o)
            far = dot(d_v[:, cc], l1[o], 1, 1)
            for j in range(per):
                h = o * per + j
                c = hcols(h)
                dm, k, q = d_v[:, c], k_v[:, c], q_v[:, c]
                w0, w1 = weights(dm, v_v[:, c])
                f = far[:, j * HD : (j + 1) * HD]
                qg_v[:top, c] = (dot(w0, k[:top], 1, 0) + f[:top]).astype(BF16)
                qg_v[top:, c] = (dot(w1, k, 1, 0) + f[top:]).astype(BF16)
                t = dot(w1, q[top:], 0, 0)
                mix[:top, c] = dot(w0, q[:top], 0, 0) + t[:top]
                mix[top:, c] = t[top:]
                t = dot(aw1[h], dm[top:], 0, 0)
                acc[:top, c] = dot(aw0[h], dm[:top], 0, 0) + t[:top]
                acc[top:, c] = t[top:]

        m1, m2 = 5, 10
        each(m1, grads)
        turn(s2, r2, s2_r, back2, p2, l2, 0, True)

        take(gs.at[0 : nc - 1], g1.at[0 : nc - 1], g1_r)
        part = g1[0]
        for c in range(1, nc):
            part = part + g1[c]
        g2s[...] = part
        g2[row] = part

        for i in range(ndp - 1):
            pltpu.make_async_remote_copy(
                src_ref=g2s, dst_ref=g2.at[row], send_sem=g2_s, recv_sem=g2_r,
                device_id={"dp": lax.rem(row + 1 + i, ndp)}, device_id_type=MESH,
            ).start()

        each(m2, grads, m1)

        take(g2.at[0 : ndp - 1], g2.at[0 : ndp - 1], g2_r)
        total = g2[0]
        for c in range(1, ndp):
            total = total + g2[c]
        g3s[...] = total
        g3[me] = total
        for i in others:
            ctx_copy(g3s, g3.at[me], g3_s, g3_r, i).start()

        for j in range(1, per):
            turn(s2, r2, s2_r, back2, p2, l2, j, True)
        each(nc, grads, m2)

        take(g3.at[0 : nc - 1], g3.at[0 : nc - 1], g3_r)
        for c in range(nc):
            gg[:, c * wid : (c + 1) * wid] = g3[c]

        for p, sem in ((s1, s1_s), (p1, p1_s), (s2, s2_s), (p2, p2_s), (g1, g1_s), (g3, g3_s)):
            take(p.at[0 : nc - 1], p.at[0 : nc - 1], sem)
        take(g2.at[0 : ndp - 1], g2.at[0 : ndp - 1], g2_s)
        take(p2.at[0 : nc - 1], p2.at[0 : nc - 1], p2_r)

    bufb = pltpu.VMEM((tok, feat), BF16)
    buff = pltpu.VMEM((tok, feat), F32)
    state = pltpu.VMEM((nc, per, HD, HD), BF16)
    square = pltpu.VMEM((nc, wid, wid), BF16)
    one = pltpu.SemaphoreType.DMA
    part = pltpu.VMEM((1, wid), F32)
    parts = pltpu.VMEM((nc, 1, wid), F32)
    return pl.pallas_call(
        kernel,
        out_shape=(bufb, bufb, buff, buff, bufb, bufb, square, pltpu.VMEM((1, feat), F32)),
        in_specs=[pl.BlockSpec(memory_space=pltpu.MemorySpace.HBM)] * 5,
        out_specs=[pl.BlockSpec(memory_space=pltpu.VMEM)] * 8,
        scratch_shapes=[
            bufb, bufb, pltpu.VMEM((1, feat), F32),
            pltpu.VMEM((heads, top, top), BF16), pltpu.VMEM((heads, low, tok), BF16),
            pltpu.VMEM((tok, HD), F32), pltpu.VMEM((tok, HD), F32),
            state, state, state, square, state, state, state,
            parts, parts, part, pltpu.VMEM((ndp, 1, wid), F32), part, parts,
            one((2, nload)), one, one, one,
            one, one((per,)), one, one((per,)), one, one((per,)), one, one,
            one, one, one, one, one, one,
        ],
        compiler_params=pltpu.CompilerParams(
            collective_id=0, has_side_effects=True, vmem_limit_bytes=32 * 2**20
        ),
        name="layer",
    )


def make_finish(tok, feat, nc):
    per = feat // HD // nc
    wid = per * HD

    def kernel(out_v, qg_v, mix, acc, k_v, v_v, l2, gg, out_h, qg_h, kg_h, vg_h, gg_o, kg_v, vg_v, sem):
        whole = [
            pltpu.make_async_copy(out_v, out_h, sem.at[0]),
            pltpu.make_async_copy(qg_v, qg_h, sem.at[1]),
            pltpu.make_async_copy(kg_v, kg_h, sem.at[2]),
            pltpu.make_async_copy(vg_v, vg_h, sem.at[3]),
        ]
        whole[0].start()
        whole[1].start()
        gg_o[...] = gg[...]

        def final(o):
            c = pl.ds(pl.multiple_of(o * wid, wid), wid)
            kg_v[:, c] = (mix[:, c] + dot(v_v[:, c], l2[o], 1, 1)).astype(BF16)
            vg_v[:, c] = (acc[:, c] + dot(k_v[:, c], l2[o], 1, 0)).astype(BF16)
            pltpu.make_async_copy(kg_v.at[:, c], kg_h.at[:, c], sem.at[2]).start()
            pltpu.make_async_copy(vg_v.at[:, c], vg_h.at[:, c], sem.at[3]).start()

        each(nc, final, unroll=2)
        for w in whole:
            w.wait()

    big = jax.ShapeDtypeStruct((tok, feat), BF16)
    bufb = pltpu.VMEM((tok, feat), BF16)
    vm = pl.BlockSpec(memory_space=pltpu.VMEM)
    return pl.pallas_call(
        kernel,
        out_shape=(big, big, big, big, jax.ShapeDtypeStruct((1, feat), F32)),
        in_specs=[vm] * 8,
        out_specs=[pl.BlockSpec(memory_space=pltpu.MemorySpace.HBM)] * 4 + [vm],
        scratch_shapes=[bufb, bufb, pltpu.SemaphoreType.DMA((4,))],
        compiler_params=pltpu.CompilerParams(vmem_limit_bytes=12 * 2**20),
        name="finish",
    )


def solution(mesh):
    nc, ndp = mesh.shape["context"], mesh.shape["dp"]

    def shards(queries, keys, values, gain, out_grad):
        tok, feat = queries.shape[1:]
        held = make_layer(tok, feat, nc, ndp)(
            queries[0], keys[0], values[0],
            pltpu.with_memory_space_constraint(gain[None], pltpu.MemorySpace.HBM), out_grad[0],
        )
        out, qg, kg, vg, gg = make_finish(tok, feat, nc)(*held)
        return out[None], qg[None], kg[None], vg[None], gg[0]

    spec = P("dp", "context", None)
    return jax.shard_map(
        shards, mesh=mesh, in_specs=(spec, spec, spec, P(), spec),
        out_specs=(spec, spec, spec, spec, P()), check_vma=False,
    )
```
